32 devices in a mesh: mem: 4 (over y, x), band: 8 (over z, core).
Axes of the slice: x: 2, y: 2, z: 4, core: 2. Of those that a mesh axis runs over, the one named last changes fastest.
Arguments:
- control: bfloat16 [16, 1440, 16, 704], P('mem', 'band'), may hold values from -6 to 6
- perturb: bfloat16 [16, 2, 16, 704, 1440], P('mem', None, None, 'band'), may hold values from -6 to 6
- loc_scales: float32 [2], replicated, may hold values from 0.0009765625 to 0.00390625
- member_of: int32 [16], replicated, may hold values from 0 to 15, as said below
Outputs:
- increment: float32 [2, 16, 704, 1440], P(None, None, 'band', 'mem')
The draws below stay inside these ranges and needn't reach their ends.
Inputs may be any that keep to these rules, and one draw needn't show every extreme that they name: member_of is a permutation, and member_of[s] // 4 == s // 4.
All inputs are finite; a program needn't handle non-finite values.
Results may differ from the reference program's by a relative error of at most 0.0053.
Values may be sent and summed in bfloat16 or wider, within the bound.
No kernel may reach another device: no remote copies, remote signals or barrier semaphores. Data moves between devices by JAX's collectives and lax.ppermute only.
A program may use at most 192 MiB of HBM per device.

```python
import math
import jax
import jax.numpy as jnp
from jax import lax

NLAT = 704
NLON = 1440
LEVELS = 16
TIMES = 2
MEM_DEV = 4
MEMBERS = 16


def draw_member_of(key, part):
    groups = MEMBERS // MEM_DEV
    keys = jax.random.split(key, groups)
    orders = jax.vmap(lambda one_key: jax.random.permutation(one_key, MEM_DEV))(keys)
    offsets = MEM_DEV * jnp.arange(groups, dtype=jnp.int32)
    return (orders.astype(jnp.int32) + offsets[:, None]).reshape(MEMBERS).astype(jnp.int32)


def steps_of(stream_key, extent, cuts, low, high):
    def one(dim, parts):
        steps = jax.random.uniform(jax.random.fold_in(jax.random.fold_in(stream_key, 6), dim), (parts,), jnp.float32, low / len(cuts), high / len(cuts))
        return jnp.repeat(jnp.exp(steps), extent[dim] // parts).reshape((-1,) + (1,) * (len(extent) - dim - 1))

    loudness = one(*cuts[0])
    for cut in cuts[1:]:
        loudness = loudness * one(*cut)
    return loudness


def gaussian(key, extent, width, reach, shards=(), held_as=jnp.bfloat16):
    entries = width * jax.random.normal(key, extent, jnp.float32)
    if shards:
        entries = entries * steps_of(key, extent, shards, -0.22, 0.18)
    return jnp.clip(entries, -reach, reach).astype(held_as)


def setup_inputs(seed: int = 0) -> dict:
    splits = jax.random.split(jax.random.key(seed), 5)
    return {
        "control": gaussian(splits[0], (MEMBERS, NLON, LEVELS, NLAT), 1.0, 6.0, ((0, 4), (1, 8))),
        "perturb": gaussian(splits[1], (MEMBERS, TIMES, LEVELS, NLAT, NLON), 1.0, 6.0, ((0, 4), (3, 8))),
        "loc_scales": jnp.clip(jnp.exp(jax.random.uniform(splits[2], (2,), jnp.float32, math.log(0.0009765625), math.log(0.00390625))), 0.0009765625, 0.00390625),
        "member_of": draw_member_of(jax.random.fold_in(splits[4], 71), 0),
    }


def kernel_matrix(cells, spread, periodic):
    index_vec = jnp.arange(cells, dtype=jnp.float32)
    distance = jnp.abs(index_vec[:, None] - index_vec[None, :])
    if periodic:
        distance = jnp.minimum(distance, cells - distance)
    weights = jnp.exp(-0.5 * (distance / spread) ** 2) / jnp.sqrt(math.sqrt(math.pi) * spread)
    return weights.astype(jnp.bfloat16)

def reference(control, perturb, loc_scales, member_of):
    lat_matrix = kernel_matrix(NLAT, loc_scales[0] * NLAT, False)
    lon_matrix = kernel_matrix(NLON, loc_scales[1] * NLON, True)

    def one_slot(running, slot_pair):
        slot_pert, member = slot_pair
        field = lax.dynamic_index_in_dim(control, member, 0, keepdims=False)
        along_lat = jnp.einsum('kla,ba->klb', field.astype(jnp.float32), lat_matrix.astype(jnp.float32)).astype(jnp.bfloat16)
        localized = jnp.einsum('kla,nk->lan', along_lat.astype(jnp.float32), lon_matrix.astype(jnp.float32))
        return (running + slot_pert.astype(jnp.float32) * localized[None], None)
    start = jnp.zeros((TIMES, LEVELS, NLAT, NLON), jnp.float32)
    summed, _ = lax.scan(one_slot, start, (perturb, member_of))
    return summed / math.sqrt(MEMBERS - 1)
```

```python
import functools
import math

import jax
import jax.numpy as jnp
from jax import lax
from jax.experimental import pallas as pl
from jax.experimental.pallas import tpu as pltpu
from jax.sharding import PartitionSpec as P

NLAT = 704
NLON = 1440
LANE = 128


def kernel_entries(rows, columns, cells, spread, periodic):
    distance = jnp.abs(rows[:, None].astype(jnp.float32) - columns[None, :].astype(jnp.float32))
    if periodic:
        distance = jnp.minimum(distance, cells - distance)
    weights = jnp.exp(-0.5 * (distance / spread) ** 2) / jnp.sqrt(math.sqrt(math.pi) * spread)
    return weights.astype(jnp.bfloat16)


def kernel_matrix(cells, spread, periodic):
    index = jnp.arange(cells, dtype=jnp.int32)
    return kernel_entries(index, index, cells, spread, periodic)


def round_up(value, unit):
    return -(-value // unit) * unit


def chunks_of(levels):
    starts = list(range(0, levels, 3))
    return [(first, min(3, levels - first)) for first in starts]


def send_kernel(first, count, base, own_ref, control_ref, lat_ref, *rest):
    outs, (held, wide, rows_ref, sems) = rest[:-4], rest[-4:]
    group, lon, block = held.shape[0], held.shape[1], held.shape[2]
    lat = outs[0].shape[0]
    tail = lon - LANE
    n_fields = group * count
    copies = [
        pltpu.make_async_copy(
            control_ref.at[own_ref[s], :, pl.ds(base, block), :], held.at[s], sems.at[s]
        )
        for s in range(group)
    ]
    for copy in copies:
        copy.start()
    used = n_fields * lon
    if rows_ref.shape[0] > used:
        rows_ref[used:, :] = jnp.zeros((rows_ref.shape[0] - used, rows_ref.shape[1]), jnp.float32)
    for s in range(group):
        copies[s].wait()
        for at in range(0, held.shape[3], LANE):
            lanes = min(LANE, held.shape[3] - at)
            wide[:, :lanes] = held[s, :, :, at : at + lanes].astype(jnp.float32).reshape(
                lon * block, lanes
            )
            for i in range(count):
                field = i * group + s
                rows = wide[pl.ds(first - base + i, lon, stride=block), :][:, :lanes]
                rows_ref[pl.ds(field * LANE, LANE), at : at + lanes] = rows[:LANE]
                rows_ref[pl.ds(n_fields * LANE + field * tail, tail), at : at + lanes] = rows[LANE:]

    def columns(start, width):
        part = rows_ref[pl.ds(start, width), :].astype(jnp.bfloat16)
        product = lax.dot_general(
            lat_ref[...], part, (((1,), (1,)), ((), ())), preferred_element_type=jnp.float32
        )
        for v, out in enumerate(outs):
            out[:, pl.ds(start, width)] = product[v * lat : (v + 1) * lat].astype(jnp.bfloat16)

    width = 2 * LANE
    whole = rows_ref.shape[0] // width

    @pl.loop(0, whole)
    def _(step):
        columns(pl.multiple_of(step * width, width), width)

    if rows_ref.shape[0] % width:
        columns(whole * width, rows_ref.shape[0] % width)


def send_parts(control, own, lat_matrix, first, count, n_band):
    group, lon, levels, nlat = control.shape
    unit = 8
    base = first // unit * unit
    block = round_up(first + count, unit) - base
    n_rows = round_up(group * count * lon, LANE)
    return pl.pallas_call(
        functools.partial(send_kernel, first, count, base),
        out_shape=[jax.ShapeDtypeStruct((nlat // n_band, n_rows), jnp.bfloat16)] * n_band,
        in_specs=[
            pl.BlockSpec(memory_space=pltpu.SMEM),
            pl.BlockSpec(memory_space=pl.ANY),
            pl.BlockSpec(memory_space=pltpu.VMEM),
        ],
        out_specs=[pl.BlockSpec(memory_space=pltpu.VMEM)] * n_band,
        scratch_shapes=[
            pltpu.VMEM((group, lon, block, nlat), jnp.bfloat16),
            pltpu.VMEM((lon * block, LANE), jnp.float32),
            pltpu.VMEM((n_rows, nlat), jnp.float32),
            pltpu.SemaphoreType.DMA((group,)),
        ],
        compiler_params=pltpu.CompilerParams(vmem_limit_bytes=56 * 2**20),
        cost_estimate=pl.CostEstimate(
            flops=2 * n_rows * nlat * nlat,
            bytes_accessed=2 * group * lon * block * nlat + 2 * n_rows * nlat,
            transcendentals=0,
        ),
        name="lat_conv",
    )(own, control, lat_matrix)


def widen_kernel(count, scale, *refs):
    n_band = len(refs) - 5
    parts, (lon_ref, perturb_ref, out_ref, lhs_ref, inc_ref) = refs[:n_band], refs[n_band:]
    group, times, lat, nlon = (perturb_ref.shape[i] for i in (0, 1, 3, 4))
    lon = lon_ref.shape[1]
    tail = lon - LANE
    n_fields = group * count
    depth = 2 * LANE
    level = pl.program_id(0)

    @pl.when(level == 0)
    def _():
        lhs_ref[...] = jnp.zeros_like(lhs_ref)

    for i in range(count):

        @pl.when(level == i)
        def _():
            for v, part in enumerate(parts):
                for s in range(group):
                    field = i * group + s
                    lhs_ref[s, :lat, v * depth : v * depth + LANE] = part[
                        :, field * LANE : (field + 1) * LANE
                    ]
                    at = n_fields * LANE + field * tail
                    lhs_ref[s, :lat, v * depth + LANE : v * depth + lon] = part[:, at : at + tail]

    rows = lhs_ref.shape[0] * lhs_ref.shape[1]

    def columns(start, width):
        fields = jnp.zeros((rows, width), jnp.float32)
        lhs = lhs_ref[...].reshape(rows, lhs_ref.shape[2])
        for v in range(n_band):
            fields += jnp.dot(
                lhs[:, v * depth : v * depth + lon],
                lon_ref[v, :, pl.ds(start, width)],
                preferred_element_type=jnp.float32,
            )
        fields = fields.reshape(group, lhs_ref.shape[1], width)[:, :lat]
        for t in range(times):
            total = perturb_ref[0, t, 0, :, pl.ds(start, width)].astype(jnp.float32) * fields[0]
            for s in range(1, group):
                total += perturb_ref[s, t, 0, :, pl.ds(start, width)].astype(jnp.float32) * fields[s]
            inc_ref[t, :, pl.ds(start, width)] = total * scale

    width = 2 * LANE
    whole = nlon // width

    @pl.loop(0, whole)
    def _(step):
        columns(pl.multiple_of(step * width, width), width)

    if nlon % width:
        columns(whole * width, nlon % width)
    share = out_ref.shape[4]
    for q in range(out_ref.shape[0]):
        for t in range(times):
            out_ref[q, t, 0] = inc_ref[t, :, q * share : (q + 1) * share].astype(out_ref.dtype)


def widen(parts, lon_matrix, perturb, first, count, n_mem, scale):
    group, times, levels, lat, nlon = perturb.shape
    n_band, n_rows = len(parts), parts[0].shape[1]
    share = nlon // n_mem
    once = pl.Buffered(1)
    return pl.pallas_call(
        functools.partial(widen_kernel, count, scale),
        out_shape=jax.ShapeDtypeStruct((n_mem, times, count, lat, share), jnp.float32),
        grid=(count,),
        in_specs=[pl.BlockSpec((lat, n_rows), lambda i: (0, 0), pipeline_mode=once)] * n_band
        + [
            pl.BlockSpec(lon_matrix.shape, lambda i: (0, 0, 0), pipeline_mode=once),
            pl.BlockSpec((group, times, 1, lat, nlon), lambda i: (0, 0, first + i, 0, 0)),
        ],
        out_specs=pl.BlockSpec((n_mem, times, 1, lat, share), lambda i: (0, 0, i, 0, 0)),
        scratch_shapes=[
            pltpu.VMEM((group, round_up(lat, 16), 2 * LANE * n_band), jnp.bfloat16),
            pltpu.VMEM((times, lat, nlon), jnp.float32),
        ],
        compiler_params=pltpu.CompilerParams(vmem_limit_bytes=56 * 2**20),
        cost_estimate=pl.CostEstimate(
            flops=2 * count * group * lat * nlon * nlon,
            bytes_accessed=2 * n_band * lat * n_rows
            + 2 * count * group * times * lat * nlon
            + 4 * count * times * lat * nlon,
            transcendentals=0,
        ),
        name="lon_conv",
    )(*parts, lon_matrix, perturb)


def plain_shards(control, perturb, loc_scales, member_of):
    lat_matrix = kernel_matrix(NLAT, loc_scales[0] * NLAT, False)
    lon_matrix = kernel_matrix(NLON, loc_scales[1] * NLON, True)
    along_lat = jnp.einsum(
        "mkla,ba->mklb", control, lat_matrix, preferred_element_type=jnp.float32
    ).astype(jnp.bfloat16)
    regrouped = lax.all_to_all(along_lat, "band", split_axis=3, concat_axis=1, tiled=True)
    widened = jnp.einsum("mkla,nk->mlan", regrouped, lon_matrix, preferred_element_type=jnp.float32)
    group_size = control.shape[0]
    members_all = member_of.shape[0]
    group_index = lax.axis_index("mem")
    own_members = (
        lax.dynamic_slice_in_dim(member_of, group_index * group_size, group_size, 0)
        - group_index * group_size
    )
    one_hot = (own_members[:, None] == jnp.arange(group_size, dtype=jnp.int32)[None, :]).astype(
        jnp.float32
    )
    slot_fields = jnp.einsum("sj,jlan->slan", one_hot, widened, precision=lax.Precision.HIGHEST)
    group_part = jnp.sum(perturb.astype(jnp.float32) * slot_fields[:, None], axis=0) / math.sqrt(
        members_all - 1
    )
    return lax.psum_scatter(group_part, "mem", scatter_dimension=3, tiled=True)


def swaps(size, mask):
    return [(i, i ^ mask) for i in range(size)]


def shards(n_mem, n_band, control, perturb, loc_scales, member_of):
    group, lon, levels, nlat = control.shape
    lat, nlon = perturb.shape[3:]
    scale = 1.0 / math.sqrt(member_of.shape[0] - 1)
    mem, band = lax.axis_index("mem"), lax.axis_index("band")
    own = lax.dynamic_slice_in_dim(member_of, mem * group, group, 0) - mem * group
    partner = jnp.arange(n_band, dtype=jnp.int32) ^ band
    lat_rows = (partner[:, None] * lat + jnp.arange(lat, dtype=jnp.int32)[None, :]).reshape(-1)
    lat_matrix = kernel_entries(
        lat_rows, jnp.arange(nlat, dtype=jnp.int32), nlat, loc_scales[0] * nlat, False
    )
    order = sorted(range(1, n_band), reverse=True)
    lon_matrix = None
    arrived, done = [], []
    chunks = chunks_of(levels)
    for c, (first, count) in enumerate(chunks):
        parts = send_parts(control, own, lat_matrix, first, count, n_band)
        if lon_matrix is None:
            scales, parts = lax.optimization_barrier((loc_scales, parts))
            lon_rows = (
                partner[:, None] * lon + jnp.arange(lon, dtype=jnp.int32)[None, :]
            ).reshape(-1)
            lon_matrix = kernel_entries(
                lon_rows, jnp.arange(nlon, dtype=jnp.int32), nlon, scales[1] * nlon, True
            ).reshape(n_band, lon, nlon)
        if c >= 2:
            parts, arrived[c - 2] = lax.optimization_barrier((parts, arrived[c - 2]))
        got = [parts[0]] + [None] * (n_band - 1)
        for v in order:
            got[v] = lax.ppermute(parts[v], "band", swaps(n_band, v))
        arrived.append(got)
    for c, (first, count) in enumerate(chunks):
        shares = widen(arrived[c], lon_matrix, perturb, first, count, n_mem, scale)
        total = lax.dynamic_index_in_dim(shares, mem, 0, keepdims=False)
        for w in range(n_mem - 1, 0, -1):
            sent = lax.dynamic_index_in_dim(shares, mem ^ w, 0, keepdims=False)
            total += lax.ppermute(sent, "mem", swaps(n_mem, w))
        done.append(total)
    return jnp.concatenate(done, axis=1)


def solution(mesh):
    n_mem, n_band = mesh.shape["mem"], mesh.shape["band"]
    in_specs = (P("mem", "band", None, None), P("mem", None, None, "band", None), P(), P())
    out_specs = P(None, None, "band", "mem")
    rows, columns = NLAT // n_band, NLON // n_band
    fits = rows % 8 == 0 and LANE < columns <= 2 * LANE and columns % 4 == 0
    local = functools.partial(shards, n_mem, n_band) if fits else plain_shards
    return jax.shard_map(local, mesh=mesh, in_specs=in_specs, out_specs=out_specs, check_vma=False)
```

```python
import functools
import math

import jax
import jax.numpy as jnp
from jax import lax
from jax.experimental import pallas as pl
from jax.experimental.pallas import tpu as pltpu
from jax.sharding import PartitionSpec as P

NLAT = 704
NLON = 1440
LANE = 128
LINK = jnp.bfloat16
COST_S, COST_T, COST_R, COST_L = 1, 1, 1, 1


def cost(us):
    return pl.CostEstimate(flops=int(1e9 * us), bytes_accessed=0, transcendentals=0)


def kernel_entries(rows, columns, cells, spread, periodic):
    distance = jnp.abs(rows[:, None].astype(jnp.float32) - columns[None, :].astype(jnp.float32))
    if periodic:
        distance = jnp.minimum(distance, cells - distance)
    weights = jnp.exp(-0.5 * (distance / spread) ** 2) / jnp.sqrt(math.sqrt(math.pi) * spread)
    return weights.astype(jnp.bfloat16)


def kernel_matrix(cells, spread, periodic):
    index = jnp.arange(cells, dtype=jnp.int32)
    return kernel_entries(index, index, cells, spread, periodic)


def round_up(value, unit):
    return -(-value // unit) * unit


def chunks_of(levels):
    counts, left = [2], levels - 4
    while left:
        counts.append(min(3, left))
        left -= counts[-1]
    counts += [1, 1]
    return [(sum(counts[:c]), count) for c, count in enumerate(counts)]


def reach_of(cells):
    return int(13.65 * cells / 256)


def send_kernel(first, count, base, n_before, own_ref, control_ref, lat_ref, *rest):
    rest = rest[n_before:]
    outs, (held, wide, rows_ref, sems) = rest[:-4], rest[-4:]
    group, lon, block = held.shape[0], held.shape[1], held.shape[2]
    lat, crossing = outs[0].shape[0], outs[-1]
    tail = lon - LANE
    n_fields = group * count
    copies = [
        pltpu.make_async_copy(
            control_ref.at[own_ref[s], :, pl.ds(base, block), :], held.at[s], sems.at[s]
        )
        for s in range(group)
    ]
    for copy in copies:
        copy.start()
    used = n_fields * lon
    if rows_ref.shape[0] > used:
        rows_ref[used:, :] = jnp.zeros((rows_ref.shape[0] - used, rows_ref.shape[1]), jnp.float32)
    for s in range(group):
        copies[s].wait()
        for at in range(0, held.shape[3], LANE):
            lanes = min(LANE, held.shape[3] - at)
            wide[:, :lanes] = held[s, :, :, at : at + lanes].astype(jnp.float32).reshape(
                lon * block, lanes
            )
            for i in range(count):
                field = i * group + s
                rows = wide[pl.ds(first - base + i, lon, stride=block), :][:, :lanes]
                rows_ref[pl.ds(field * LANE, LANE), at : at + lanes] = rows[:LANE]
                rows_ref[pl.ds(n_fields * LANE + field * tail, tail), at : at + lanes] = rows[LANE:]

    def columns(start, width):
        part = rows_ref[pl.ds(start, width), :].astype(jnp.bfloat16)
        product = lax.dot_general(
            lat_ref[...], part, (((1,), (1,)), ((), ())), preferred_element_type=jnp.float32
        )
        for k, out in enumerate(outs[:-1]):
            out[:, pl.ds(start, width)] = product[k * lat : (k + 1) * lat].astype(jnp.bfloat16)
            at = (len(outs) - 1 + k) * lat
            crossing[k, :, pl.ds(start, width)] = product[at : at + lat].astype(jnp.bfloat16)

    width = 2 * LANE
    whole = rows_ref.shape[0] // width

    @pl.loop(0, whole)
    def _(step):
        columns(pl.multiple_of(step * width, width), width)

    if rows_ref.shape[0] % width:
        columns(whole * width, rows_ref.shape[0] % width)


def send_parts(control, own, lat_matrix, first, count, n_pairs, before):
    group, lon, levels, nlat = control.shape
    lat, unit = nlat // (2 * n_pairs), 8
    base = first // unit * unit
    block = round_up(first + count, unit) - base
    n_rows = round_up(group * count * lon, LANE)
    return pl.pallas_call(
        functools.partial(send_kernel, first, count, base, len(before)),
        out_shape=[jax.ShapeDtypeStruct((lat, n_rows), jnp.bfloat16)] * n_pairs
        + [jax.ShapeDtypeStruct((n_pairs, lat, n_rows), jnp.bfloat16)],
        in_specs=[
            pl.BlockSpec(memory_space=pltpu.SMEM),
            pl.BlockSpec(memory_space=pl.ANY),
            pl.BlockSpec(memory_space=pltpu.VMEM),
        ]
        + [pl.BlockSpec(memory_space=pl.ANY)] * len(before),
        out_specs=[pl.BlockSpec(memory_space=pltpu.VMEM)] * (n_pairs + 1),
        scratch_shapes=[
            pltpu.VMEM((group, lon, block, nlat), jnp.bfloat16),
            pltpu.VMEM((lon * block, LANE), jnp.float32),
            pltpu.VMEM((n_rows, nlat), jnp.float32),
            pltpu.SemaphoreType.DMA((group,)),
        ],
        compiler_params=pltpu.CompilerParams(vmem_limit_bytes=56 * 2**20),
        cost_estimate=cost(COST_S),
        name="lat_conv",
    )(own, control, lat_matrix, *before)


def merge_kernel(n_messages, n_terms, n_before, *refs):
    own, swapped, terms = refs[:n_messages], refs[n_messages], refs[n_messages + 1 :][:n_terms]
    messages = refs[n_messages + 1 + n_terms + n_before :][:n_messages]
    for k, message in enumerate(messages):
        message[0] = own[k][...]
        message[1] = swapped[k + 1]
    if n_terms:
        total = terms[0][...].astype(jnp.float32)
        for term in terms[1:]:
            total += term[...].astype(jnp.float32)
        refs[-1][...] = total


def merge(own, swapped, terms, before):
    n_messages = len(own)
    lat, n_rows = own[0].shape
    vmem = pl.BlockSpec(memory_space=pltpu.VMEM)
    outs = pl.pallas_call(
        functools.partial(merge_kernel, n_messages, len(terms), len(before)),
        out_shape=[jax.ShapeDtypeStruct((2, lat, n_rows), jnp.bfloat16)] * n_messages
        + [jax.ShapeDtypeStruct(term.shape, jnp.float32) for term in terms[:1]],
        in_specs=[vmem] * (n_messages + 1 + len(terms))
        + [pl.BlockSpec(memory_space=pl.ANY)] * len(before),
        out_specs=[vmem] * (n_messages + len(terms[:1])),
        compiler_params=pltpu.CompilerParams(vmem_limit_bytes=40 * 2**20),
        cost_estimate=cost(COST_T),
        name="merge",
    )(*own, swapped, *terms, *before)
    return list(outs[:n_messages]), list(outs[n_messages:])


def widen_kernel(count, scale, n_before, n_mem, place_ref, *refs):
    refs = refs[n_before:]
    lhs_ref, inc_ref = refs[-2:]
    outs, refs = refs[-2 - n_mem : -2], refs[: -2 - n_mem]
    parts, (own, swapped, lon_ref, perturb_ref) = refs[:-4], refs[-4:]
    n_pairs = len(parts) + 1
    group, times, lat, nlon = (perturb_ref.shape[i] for i in (0, 1, 3, 4))
    n_band, depth = 2 * n_pairs, 2 * LANE
    lon = nlon // n_band
    tail = lon - LANE
    n_fields = group * count
    level = pl.program_id(0)

    @pl.when(level == 0)
    def _():
        lhs_ref[...] = jnp.zeros_like(lhs_ref)

    for i in range(count):

        @pl.when(level == i)
        def _():
            for v in range(n_band):
                part = parts[v // 2 - 1].at[v % 2] if v > 1 else swapped.at[0] if v else own
                source = pl.multiple_of((place_ref[0] ^ v) * depth, depth)
                for s in range(group):
                    field = i * group + s
                    lhs_ref[s, :lat, pl.ds(source, LANE)] = part[
                        :, field * LANE : (field + 1) * LANE
                    ]
                    at = n_fields * LANE + field * tail
                    lhs_ref[s, :lat, pl.ds(source + LANE, tail)] = part[:, at : at + tail]

    rows = lhs_ref.shape[0] * lhs_ref.shape[1]
    reach, width = reach_of(nlon), 2 * LANE
    for start in range(0, nlon, width):
        stop = min(start + width, nlon)
        near = {(k % nlon) // lon for k in range(start - reach, stop + reach)}
        fields = jnp.zeros((rows, stop - start), jnp.float32)
        for j in sorted(near):
            fields += jnp.dot(
                lhs_ref[:, :, j * depth : (j + 1) * depth].reshape(rows, depth),
                lon_ref[j, :, start:stop],
                preferred_element_type=jnp.float32,
            )
        fields = fields.reshape(group, lhs_ref.shape[1], stop - start)[:, :lat]
        for t in range(times):
            total = perturb_ref[0, t, 0, :, start:stop].astype(jnp.float32) * fields[0]
            for s in range(1, group):
                total += perturb_ref[s, t, 0, :, start:stop].astype(jnp.float32) * fields[s]
            inc_ref[t, :, start:stop] = total * scale
    share = nlon // n_mem
    for w, out in enumerate(outs):
        for q in range(n_mem):

            @pl.when((place_ref[1] ^ w) == q)
            def _():
                for t in range(times):
                    out[t, 0] = inc_ref[t, :, q * share : (q + 1) * share].astype(out.dtype)


def widen(parts, own, swapped, place, lon_matrix, perturb, first, count, n_mem, scale, before, us):
    group, times, levels, lat, nlon = perturb.shape
    n_pairs, n_rows = len(parts) + 1, own.shape[1]
    share = nlon // n_mem
    once = pl.Buffered(1)
    return pl.pallas_call(
        functools.partial(widen_kernel, count, scale, len(before), n_mem),
        out_shape=[jax.ShapeDtypeStruct((times, count, lat, share), LINK)] * n_mem,
        grid=(count,),
        in_specs=[pl.BlockSpec(memory_space=pltpu.SMEM)]
        + [pl.BlockSpec(memory_space=pl.ANY)] * len(before)
        + [pl.BlockSpec((2, lat, n_rows), lambda i: (0, 0, 0), pipeline_mode=once)] * len(parts)
        + [
            pl.BlockSpec((lat, n_rows), lambda i: (0, 0), pipeline_mode=once),
            pl.BlockSpec((1, lat, n_rows), lambda i: (0, 0, 0), pipeline_mode=once),
            pl.BlockSpec(lon_matrix.shape, lambda i: (0, 0, 0), pipeline_mode=once),
            pl.BlockSpec((group, times, 1, lat, nlon), lambda i: (0, 0, first + i, 0, 0)),
        ],
        out_specs=[pl.BlockSpec((times, 1, lat, share), lambda i: (0, i, 0, 0))] * n_mem,
        scratch_shapes=[
            pltpu.VMEM((group, round_up(lat, 16), 4 * LANE * n_pairs), jnp.bfloat16),
            pltpu.VMEM((times, lat, nlon), jnp.float32),
        ],
        compiler_params=pltpu.CompilerParams(vmem_limit_bytes=56 * 2**20),
        cost_estimate=cost(us),
        name="lon_conv",
    )(place, *before, *parts, own, swapped, lon_matrix, perturb)


def plain_shards(control, perturb, loc_scales, member_of):
    lat_matrix = kernel_matrix(NLAT, loc_scales[0] * NLAT, False)
    lon_matrix = kernel_matrix(NLON, loc_scales[1] * NLON, True)
    along_lat = jnp.einsum(
        "mkla,ba->mklb", control, lat_matrix, preferred_element_type=jnp.float32
    ).astype(jnp.bfloat16)
    regrouped = lax.all_to_all(along_lat, "band", split_axis=3, concat_axis=1, tiled=True)
    widened = jnp.einsum("mkla,nk->mlan", regrouped, lon_matrix, preferred_element_type=jnp.float32)
    group_size = control.shape[0]
    members_all = member_of.shape[0]
    group_index = lax.axis_index("mem")
    own_members = (
        lax.dynamic_slice_in_dim(member_of, group_index * group_size, group_size, 0)
        - group_index * group_size
    )
    one_hot = (own_members[:, None] == jnp.arange(group_size, dtype=jnp.int32)[None, :]).astype(
        jnp.float32
    )
    slot_fields = jnp.einsum("sj,jlan->slan", one_hot, widened, precision=lax.Precision.HIGHEST)
    group_part = jnp.sum(perturb.astype(jnp.float32) * slot_fields[:, None], axis=0) / math.sqrt(
        members_all - 1
    )
    return lax.psum_scatter(group_part, "mem", scatter_dimension=3, tiled=True)


def swaps(size, mask):
    return [(i, i ^ mask) for i in range(size)]


def shards(n_mem, n_band, control, perturb, loc_scales, member_of):
    group, lon, levels, nlat = control.shape
    lat, nlon = perturb.shape[3:]
    n_pairs = n_band // 2
    scale = 1.0 / math.sqrt(member_of.shape[0] - 1)
    mem, band = lax.axis_index("mem"), lax.axis_index("band")
    own = lax.dynamic_slice_in_dim(member_of, mem * group, group, 0) - mem * group
    pairs = 2 * jnp.arange(n_pairs, dtype=jnp.int32)
    partner = jnp.concatenate([pairs, pairs + 1]) ^ band
    lat_rows = (partner[:, None] * lat + jnp.arange(lat, dtype=jnp.int32)[None, :]).reshape(-1)
    lat_matrix = kernel_entries(
        lat_rows, jnp.arange(nlat, dtype=jnp.int32), nlat, loc_scales[0] * nlat, False
    )
    chunks = chunks_of(levels)
    columns = jnp.arange(2 * LANE, dtype=jnp.int32)[None, :]
    sources = jnp.arange(n_band, dtype=jnp.int32)[:, None] * lon + columns
    lon_matrix = None
    prepared, arrived, made, done = [], [], [], [None] * len(chunks)
    queued = []
    ahead = 2
    place = jnp.stack([band, mem])
    for step in range(len(chunks) + ahead):
        c = step - ahead
        if step < len(chunks):
            before = queued[step - ahead][:1] if step >= ahead else []
            *own_parts, crossing = send_parts(
                control, own, lat_matrix, *chunks[step], n_pairs, before
            )
            prepared.append(own_parts)
            with jax.named_scope(f"cores_{step}"):
                swapped = lax.ppermute(crossing, "band", swaps(n_band, 1))
            early = step - ahead - 1
            messages, total = merge(
                own_parts[1:],
                swapped,
                made[early] if early >= 0 else [],
                arrived[step - ahead][0] if step >= ahead else [],
            )
            queued.append(messages)
            if early >= 0:
                done[early] = total[0]
            got = [None] * len(messages)
            for k in sorted(range(1, n_pairs), key=lambda k: -k):
                with jax.named_scope(f"chips_{step}_{k}"):
                    got[k - 1] = lax.ppermute(messages[k - 1], "band", swaps(n_band, 2 * k))
            arrived.append([got, own_parts[0], swapped])
        if c >= 0:
            if lon_matrix is None:
                scales, queued[1][0] = lax.optimization_barrier((loc_scales, queued[1][0]))
                lon_matrix = kernel_entries(
                    sources.reshape(-1),
                    jnp.arange(nlon, dtype=jnp.int32),
                    nlon,
                    scales[1] * nlon,
                    True,
                ).reshape(n_band, 2 * LANE, nlon)
                lon_matrix = jnp.where(columns[:, :, None] < lon, lon_matrix, jnp.bfloat16(0))
            before = queued[-1][:1]
            before = before + [terms[0] for terms in made[-1:]]
            shares = widen(
                *arrived[c], place, lon_matrix, perturb, *chunks[c], n_mem, scale, before,
                COST_L if c + 1 == len(chunks) else COST_R
            )
            terms = [shares[0]]
            for w in range(n_mem - 1, 0, -1):
                with jax.named_scope(f"mem_{c}_{w}"):
                    terms.append(lax.ppermute(shares[w], "mem", swaps(n_mem, w)))
            made.append(terms)
    for c, terms in enumerate(made):
        if done[c] is None:
            done[c] = sum(term.astype(jnp.float32) for term in terms)
    return jnp.concatenate(done, axis=1)


def solution(mesh):
    n_mem, n_band = mesh.shape["mem"], mesh.shape["band"]
    in_specs = (P("mem", "band", None, None), P("mem", None, None, "band", None), P(), P())
    out_specs = P(None, None, "band", "mem")
    rows, columns = NLAT // n_band, NLON // n_band
    fits = rows % 8 == 0 and LANE < columns <= 2 * LANE and columns % 4 == 0
    local = functools.partial(shards, n_mem, n_band) if fits else plain_shards
    return jax.shard_map(local, mesh=mesh, in_specs=in_specs, out_specs=out_specs, check_vma=False)
```

```python
import functools
import math

import jax
import jax.numpy as jnp
from jax import lax
from jax.experimental import pallas as pl
from jax.experimental.pallas import tpu as pltpu
from jax.sharding import PartitionSpec as P

NLAT = 704
NLON = 1440
LANE = 128
LINK = jnp.bfloat16


def little():
    return pl.CostEstimate(flops=10**9, bytes_accessed=0, transcendentals=0)


def kernel_entries(rows, columns, cells, spread, periodic):
    distance = jnp.abs(rows[:, None].astype(jnp.float32) - columns[None, :].astype(jnp.float32))
    if periodic:
        distance = jnp.minimum(distance, cells - distance)
    weights = jnp.exp(-0.5 * (distance / spread) ** 2) / jnp.sqrt(math.sqrt(math.pi) * spread)
    return weights.astype(jnp.bfloat16)


def kernel_matrix(cells, spread, periodic):
    index = jnp.arange(cells, dtype=jnp.int32)
    return kernel_entries(index, index, cells, spread, periodic)


def round_up(value, unit):
    return -(-value // unit) * unit


def chunks_of(levels):
    counts, left = [2], levels - 4
    while left:
        counts.append(min(3, left))
        left -= counts[-1]
    counts += [1, 1]
    return [(sum(counts[:c]), count) for c, count in enumerate(counts)]


def partner_order(n_pairs):
    return [*range(2, n_pairs), 1]


def reach_of(cells):
    return int(13.65 * cells / 256)


def send_kernel(first, count, base, n_before, own_ref, control_ref, lat_ref, *rest):
    rest = rest[n_before:]
    outs, (held, wide, rows_ref, sems) = rest[:-4], rest[-4:]
    group, lon, block = held.shape[0], held.shape[1], held.shape[2]
    lat, crossing = outs[0].shape[0], outs[-1]
    tail = lon - LANE
    n_fields = group * count
    copies = [
        pltpu.make_async_copy(
            control_ref.at[own_ref[s], :, pl.ds(base, block), :], held.at[s], sems.at[s]
        )
        for s in range(group)
    ]
    for copy in copies:
        copy.start()
    used = n_fields * lon
    if rows_ref.shape[0] > used:
        rows_ref[used:, :] = jnp.zeros((rows_ref.shape[0] - used, rows_ref.shape[1]), jnp.float32)
    for s in range(group):
        copies[s].wait()
        for at in range(0, held.shape[3], LANE):
            lanes = min(LANE, held.shape[3] - at)
            wide[:, :lanes] = held[s, :, :, at : at + lanes].astype(jnp.float32).reshape(
                lon * block, lanes
            )
            for i in range(count):
                field = i * group + s
                rows = wide[pl.ds(first - base + i, lon, stride=block), :][:, :lanes]
                rows_ref[pl.ds(field * LANE, LANE), at : at + lanes] = rows[:LANE]
                rows_ref[pl.ds(n_fields * LANE + field * tail, tail), at : at + lanes] = rows[LANE:]

    def columns(start, width):
        part = rows_ref[pl.ds(start, width), :].astype(jnp.bfloat16)
        product = lax.dot_general(
            lat_ref[...], part, (((1,), (1,)), ((), ())), preferred_element_type=jnp.float32
        )
        for k, out in enumerate(outs[:-1]):
            out[:, pl.ds(start, width)] = product[k * lat : (k + 1) * lat].astype(jnp.bfloat16)
            at = (len(outs) - 1 + k) * lat
            crossing[k, :, pl.ds(start, width)] = product[at : at + lat].astype(jnp.bfloat16)

    width = 2 * LANE
    whole = rows_ref.shape[0] // width

    @pl.loop(0, whole)
    def _(step):
        columns(pl.multiple_of(step * width, width), width)

    if rows_ref.shape[0] % width:
        columns(whole * width, rows_ref.shape[0] % width)


def send_parts(control, own, lat_matrix, first, count, n_pairs, before):
    group, lon, levels, nlat = control.shape
    lat, unit = nlat // (2 * n_pairs), 8
    base = first // unit * unit
    block = round_up(first + count, unit) - base
    n_rows = round_up(group * count * lon, LANE)
    return pl.pallas_call(
        functools.partial(send_kernel, first, count, base, len(before)),
        out_shape=[jax.ShapeDtypeStruct((lat, n_rows), jnp.bfloat16)] * n_pairs
        + [jax.ShapeDtypeStruct((n_pairs, lat, n_rows), jnp.bfloat16)],
        in_specs=[
            pl.BlockSpec(memory_space=pltpu.SMEM),
            pl.BlockSpec(memory_space=pl.ANY),
            pl.BlockSpec(memory_space=pltpu.VMEM),
        ]
        + [pl.BlockSpec(memory_space=pl.ANY)] * len(before),
        out_specs=[pl.BlockSpec(memory_space=pltpu.VMEM)] * (n_pairs + 1),
        scratch_shapes=[
            pltpu.VMEM((group, lon, block, nlat), jnp.bfloat16),
            pltpu.VMEM((lon * block, LANE), jnp.float32),
            pltpu.VMEM((n_rows, nlat), jnp.float32),
            pltpu.SemaphoreType.DMA((group,)),
        ],
        compiler_params=pltpu.CompilerParams(vmem_limit_bytes=56 * 2**20),
        cost_estimate=little(),
        name="lat_conv",
    )(own, control, lat_matrix, *before)


def merge_kernel(n_messages, n_terms, n_before, *refs):
    own, swapped, terms = refs[:n_messages], refs[n_messages], refs[n_messages + 1 :][:n_terms]
    messages = refs[n_messages + 1 + n_terms + n_before :][:n_messages]
    for i, k in enumerate(partner_order(n_messages + 1)):
        messages[i][0] = own[i][...]
        messages[i][1] = swapped[k]
    if n_terms:
        total = terms[0][...].astype(jnp.float32)
        for term in terms[1:]:
            total += term[...].astype(jnp.float32)
        refs[-1][...] = total


def merge(own, swapped, terms, before):
    n_messages = len(own)
    lat, n_rows = own[0].shape
    vmem = pl.BlockSpec(memory_space=pltpu.VMEM)
    outs = pl.pallas_call(
        functools.partial(merge_kernel, n_messages, len(terms), len(before)),
        out_shape=[jax.ShapeDtypeStruct((2, lat, n_rows), jnp.bfloat16)] * n_messages
        + [jax.ShapeDtypeStruct(term.shape, jnp.float32) for term in terms[:1]],
        in_specs=[vmem] * (n_messages + 1 + len(terms))
        + [pl.BlockSpec(memory_space=pl.ANY)] * len(before),
        out_specs=[vmem] * (n_messages + len(terms[:1])),
        compiler_params=pltpu.CompilerParams(vmem_limit_bytes=40 * 2**20),
        cost_estimate=little(),
        name="merge",
    )(*own, swapped, *terms, *before)
    return list(outs[:n_messages]), list(outs[n_messages:])


def widen_kernel(count, scale, n_before, n_mem, place_ref, *refs):
    refs = refs[n_before:]
    lhs_ref, inc_ref = refs[-2:]
    outs, refs = refs[-2 - n_mem : -2], refs[: -2 - n_mem]
    parts, (own, swapped, lon_ref, perturb_ref) = refs[:-4], refs[-4:]
    n_pairs = len(parts) + 1
    order = partner_order(n_pairs)
    group, times, lat, nlon = (perturb_ref.shape[i] for i in (0, 1, 3, 4))
    n_band, depth = 2 * n_pairs, 2 * LANE
    lon = nlon // n_band
    tail = lon - LANE
    n_fields = group * count
    level = pl.program_id(0)

    @pl.when(level == 0)
    def _():
        lhs_ref[...] = jnp.zeros_like(lhs_ref)

    for i in range(count):

        @pl.when(level == i)
        def _():
            for v in range(n_band):
                part = parts[order.index(v // 2)].at[v % 2] if v > 1 else swapped.at[0] if v else own
                source = pl.multiple_of((place_ref[0] ^ v) * depth, depth)
                for s in range(group):
                    field = i * group + s
                    lhs_ref[s, :lat, pl.ds(source, LANE)] = part[
                        :, field * LANE : (field + 1) * LANE
                    ]
                    at = n_fields * LANE + field * tail
                    lhs_ref[s, :lat, pl.ds(source + LANE, tail)] = part[:, at : at + tail]

    rows = lhs_ref.shape[0] * lhs_ref.shape[1]
    reach, width = reach_of(nlon), 2 * LANE
    for start in range(0, nlon, width):
        stop = min(start + width, nlon)
        near = {(k % nlon) // lon for k in range(start - reach, stop + reach)}
        fields = jnp.zeros((rows, stop - start), jnp.float32)
        for j in sorted(near):
            fields += jnp.dot(
                lhs_ref[:, :, j * depth : (j + 1) * depth].reshape(rows, depth),
                lon_ref[j, :, start:stop],
                preferred_element_type=jnp.float32,
            )
        fields = fields.reshape(group, lhs_ref.shape[1], stop - start)[:, :lat]
        for t in range(times):
            total = perturb_ref[0, t, 0, :, start:stop].astype(jnp.float32) * fields[0]
            for s in range(1, group):
                total += perturb_ref[s, t, 0, :, start:stop].astype(jnp.float32) * fields[s]
            inc_ref[t, :, start:stop] = total * scale
    share = nlon // n_mem
    for w, out in enumerate(outs):
        for q in range(n_mem):

            @pl.when((place_ref[1] ^ w) == q)
            def _():
                for t in range(times):
                    out[t, 0] = inc_ref[t, :, q * share : (q + 1) * share].astype(out.dtype)


def widen(parts, own, swapped, place, lon_matrix, perturb, first, count, n_mem, scale, before):
    group, times, levels, lat, nlon = perturb.shape
    n_pairs, n_rows = len(parts) + 1, own.shape[1]
    share = nlon // n_mem
    once = pl.Buffered(1)
    return pl.pallas_call(
        functools.partial(widen_kernel, count, scale, len(before), n_mem),
        out_shape=[jax.ShapeDtypeStruct((times, count, lat, share), LINK)] * n_mem,
        grid=(count,),
        in_specs=[pl.BlockSpec(memory_space=pltpu.SMEM)]
        + [pl.BlockSpec(memory_space=pl.ANY)] * len(before)
        + [pl.BlockSpec((2, lat, n_rows), lambda i: (0, 0, 0), pipeline_mode=once)] * len(parts)
        + [
            pl.BlockSpec((lat, n_rows), lambda i: (0, 0), pipeline_mode=once),
            pl.BlockSpec((1, lat, n_rows), lambda i: (0, 0, 0), pipeline_mode=once),
            pl.BlockSpec(lon_matrix.shape, lambda i: (0, 0, 0), pipeline_mode=once),
            pl.BlockSpec((group, times, 1, lat, nlon), lambda i: (0, 0, first + i, 0, 0)),
        ],
        out_specs=[pl.BlockSpec((times, 1, lat, share), lambda i: (0, i, 0, 0))] * n_mem,
        scratch_shapes=[
            pltpu.VMEM((group, round_up(lat, 16), 4 * LANE * n_pairs), jnp.bfloat16),
            pltpu.VMEM((times, lat, nlon), jnp.float32),
        ],
        compiler_params=pltpu.CompilerParams(vmem_limit_bytes=56 * 2**20),
        cost_estimate=little(),
        name="lon_conv",
    )(place, *before, *parts, own, swapped, lon_matrix, perturb)


def plain_shards(control, perturb, loc_scales, member_of):
    lat_matrix = kernel_matrix(NLAT, loc_scales[0] * NLAT, False)
    lon_matrix = kernel_matrix(NLON, loc_scales[1] * NLON, True)
    along_lat = jnp.einsum(
        "mkla,ba->mklb", control, lat_matrix, preferred_element_type=jnp.float32
    ).astype(jnp.bfloat16)
    regrouped = lax.all_to_all(along_lat, "band", split_axis=3, concat_axis=1, tiled=True)
    widened = jnp.einsum("mkla,nk->mlan", regrouped, lon_matrix, preferred_element_type=jnp.float32)
    group_size = control.shape[0]
    members_all = member_of.shape[0]
    group_index = lax.axis_index("mem")
    own_members = (
        lax.dynamic_slice_in_dim(member_of, group_index * group_size, group_size, 0)
        - group_index * group_size
    )
    one_hot = (own_members[:, None] == jnp.arange(group_size, dtype=jnp.int32)[None, :]).astype(
        jnp.float32
    )
    slot_fields = jnp.einsum("sj,jlan->slan", one_hot, widened, precision=lax.Precision.HIGHEST)
    group_part = jnp.sum(perturb.astype(jnp.float32) * slot_fields[:, None], axis=0) / math.sqrt(
        members_all - 1
    )
    return lax.psum_scatter(group_part, "mem", scatter_dimension=3, tiled=True)


def swaps(size, mask):
    return [(i, i ^ mask) for i in range(size)]


def shards(n_mem, n_band, control, perturb, loc_scales, member_of):
    group, lon, levels, nlat = control.shape
    lat, nlon = perturb.shape[3:]
    n_pairs = n_band // 2
    scale = 1.0 / math.sqrt(member_of.shape[0] - 1)
    mem, band = lax.axis_index("mem"), lax.axis_index("band")
    own = lax.dynamic_slice_in_dim(member_of, mem * group, group, 0) - mem * group
    pairs = 2 * jnp.arange(n_pairs, dtype=jnp.int32)
    partner = jnp.concatenate([pairs, pairs + 1]) ^ band
    lat_rows = (partner[:, None] * lat + jnp.arange(lat, dtype=jnp.int32)[None, :]).reshape(-1)
    lat_matrix = kernel_entries(
        lat_rows, jnp.arange(nlat, dtype=jnp.int32), nlat, loc_scales[0] * nlat, False
    )
    chunks = chunks_of(levels)
    columns = jnp.arange(2 * LANE, dtype=jnp.int32)[None, :]
    sources = jnp.arange(n_band, dtype=jnp.int32)[:, None] * lon + columns
    lon_matrix = None
    prepared, arrived, made, done = [], [], [], [None] * len(chunks)
    queued = []
    order = partner_order(n_pairs)
    ahead = 2
    place = jnp.stack([band, mem])
    for step in range(len(chunks) + ahead):
        c = step - ahead
        if step < len(chunks):
            before = queued[step - ahead][:1] if step >= ahead else []
            *own_parts, crossing = send_parts(
                control, own, lat_matrix, *chunks[step], n_pairs, before
            )
            prepared.append(own_parts)
            with jax.named_scope(f"cores_{step}"):
                swapped = lax.ppermute(crossing, "band", swaps(n_band, 1))
            early = step - ahead - 1
            messages, total = merge(
                [own_parts[k] for k in order],
                swapped,
                made[early] if early >= 0 else [],
                arrived[step - ahead][0] if step >= ahead else [],
            )
            queued.append(messages)
            if early >= 0:
                done[early] = total[0]
            got = []
            for k, message in zip(order, messages):
                with jax.named_scope(f"chips_{step}_{k}"):
                    got.append(lax.ppermute(message, "band", swaps(n_band, 2 * k)))
            arrived.append([got, own_parts[0], swapped])
        if c >= 0:
            if lon_matrix is None:
                scales, queued[1][0] = lax.optimization_barrier((loc_scales, queued[1][0]))
                lon_matrix = kernel_entries(
                    sources.reshape(-1),
                    jnp.arange(nlon, dtype=jnp.int32),
                    nlon,
                    scales[1] * nlon,
                    True,
                ).reshape(n_band, 2 * LANE, nlon)
                lon_matrix = jnp.where(columns[:, :, None] < lon, lon_matrix, jnp.bfloat16(0))
            before = queued[-1][:1]
            before = before + [terms[0] for terms in made[-1:]]
            shares = widen(
                *arrived[c], place, lon_matrix, perturb, *chunks[c], n_mem, scale, before
            )
            terms = [shares[0]]
            for w in range(n_mem - 1, 0, -1):
                with jax.named_scope(f"mem_{c}_{w}"):
                    terms.append(lax.ppermute(shares[w], "mem", swaps(n_mem, w)))
            made.append(terms)
    for c, terms in enumerate(made):
        if done[c] is None:
            done[c] = sum(term.astype(jnp.float32) for term in terms)
    return jnp.concatenate(done, axis=1)


def solution(mesh):
    n_mem, n_band = mesh.shape["mem"], mesh.shape["band"]
    in_specs = (P("mem", "band", None, None), P("mem", None, None, "band", None), P(), P())
    out_specs = P(None, None, "band", "mem")
    rows, columns = NLAT // n_band, NLON // n_band
    fits = n_band >= 4 and rows % 8 == 0 and LANE < columns <= 2 * LANE and columns % 4 == 0
    local = functools.partial(shards, n_mem, n_band) if fits else plain_shards
    return jax.shard_map(local, mesh=mesh, in_specs=in_specs, out_specs=out_specs, check_vma=False)
```

```python
import functools
import math

import jax
import jax.numpy as jnp
from jax import lax
from jax.experimental import pallas as pl
from jax.experimental.pallas import tpu as pltpu
from jax.sharding import PartitionSpec as P

NLAT = 704
NLON = 1440
LANE = 128
LINK = jnp.bfloat16
COST_S, COST_T, COST_R, COST_L = 1, 1, 1, 1


def cost(us):
    return pl.CostEstimate(flops=int(1e9 * us), bytes_accessed=0, transcendentals=0)


def kernel_entries(rows, columns, cells, spread, periodic):
    distance = jnp.abs(rows[:, None].astype(jnp.float32) - columns[None, :].astype(jnp.float32))
    if periodic:
        distance = jnp.minimum(distance, cells - distance)
    weights = jnp.exp(-0.5 * (distance / spread) ** 2) / jnp.sqrt(math.sqrt(math.pi) * spread)
    return weights.astype(jnp.bfloat16)


def kernel_matrix(cells, spread, periodic):
    index = jnp.arange(cells, dtype=jnp.int32)
    return kernel_entries(index, index, cells, spread, periodic)


def round_up(value, unit):
    return -(-value // unit) * unit


def chunks_of(levels):
    counts, left = [2], levels - 4
    while left:
        counts.append(min(3, left))
        left -= counts[-1]
    counts += [1, 1]
    return [(sum(counts[:c]), count) for c, count in enumerate(counts)]


def reach_of(cells):
    return int(13.65 * cells / 256)


def send_kernel(first, count, base, n_before, own_ref, control_ref, lat_ref, *rest):
    rest = rest[n_before:]
    outs, (held, wide, rows_ref, sems) = rest[:-4], rest[-4:]
    group, lon, block = held.shape[0], held.shape[1], held.shape[2]
    lat, crossing = outs[0].shape[0], outs[-1]
    tail = lon - LANE
    n_fields = group * count
    copies = [
        pltpu.make_async_copy(
            control_ref.at[own_ref[s], :, pl.ds(base, block), :], held.at[s], sems.at[s]
        )
        for s in range(group)
    ]
    for copy in copies:
        copy.start()
    used = n_fields * lon
    if rows_ref.shape[0] > used:
        rows_ref[used:, :] = jnp.zeros((rows_ref.shape[0] - used, rows_ref.shape[1]), jnp.float32)
    for s in range(group):
        copies[s].wait()
        for at in range(0, held.shape[3], LANE):
            lanes = min(LANE, held.shape[3] - at)
            wide[:, :lanes] = held[s, :, :, at : at + lanes].astype(jnp.float32).reshape(
                lon * block, lanes
            )
            for i in range(count):
                field = i * group + s
                rows = wide[pl.ds(first - base + i, lon, stride=block), :][:, :lanes]
                rows_ref[pl.ds(field * LANE, LANE), at : at + lanes] = rows[:LANE]
                rows_ref[pl.ds(n_fields * LANE + field * tail, tail), at : at + lanes] = rows[LANE:]

    def columns(start, width):
        part = rows_ref[pl.ds(start, width), :].astype(jnp.bfloat16)
        product = lax.dot_general(
            lat_ref[...], part, (((1,), (1,)), ((), ())), preferred_element_type=jnp.float32
        )
        for k, out in enumerate(outs[:-1]):
            out[:, pl.ds(start, width)] = product[k * lat : (k + 1) * lat].astype(jnp.bfloat16)
            at = (len(outs) - 1 + k) * lat
            crossing[k, :, pl.ds(start, width)] = product[at : at + lat].astype(jnp.bfloat16)

    width = 2 * LANE
    whole = rows_ref.shape[0] // width

    @pl.loop(0, whole)
    def _(step):
        columns(pl.multiple_of(step * width, width), width)

    if rows_ref.shape[0] % width:
        columns(whole * width, rows_ref.shape[0] % width)


def send_parts(control, own, lat_matrix, first, count, n_pairs, before):
    group, lon, levels, nlat = control.shape
    lat, unit = nlat // (2 * n_pairs), 8
    base = first // unit * unit
    block = round_up(first + count, unit) - base
    n_rows = round_up(group * count * lon, LANE)
    return pl.pallas_call(
        functools.partial(send_kernel, first, count, base, len(before)),
        out_shape=[jax.ShapeDtypeStruct((lat, n_rows), jnp.bfloat16)] * n_pairs
        + [jax.ShapeDtypeStruct((n_pairs, lat, n_rows), jnp.bfloat16)],
        in_specs=[
            pl.BlockSpec(memory_space=pltpu.SMEM),
            pl.BlockSpec(memory_space=pl.ANY),
            pl.BlockSpec(memory_space=pltpu.VMEM),
        ]
        + [pl.BlockSpec(memory_space=pl.ANY)] * len(before),
        out_specs=[pl.BlockSpec(memory_space=pltpu.VMEM)] * (n_pairs + 1),
        scratch_shapes=[
            pltpu.VMEM((group, lon, block, nlat), jnp.bfloat16),
            pltpu.VMEM((lon * block, LANE), jnp.float32),
            pltpu.VMEM((n_rows, nlat), jnp.float32),
            pltpu.SemaphoreType.DMA((group,)),
        ],
        compiler_params=pltpu.CompilerParams(vmem_limit_bytes=30 * 2**20),
        cost_estimate=cost(COST_S),
        name="lat_conv",
    )(own, control, lat_matrix, *before)


def merge_kernel(n_messages, n_terms, n_before, *refs):
    own, swapped, terms = refs[:n_messages], refs[n_messages], refs[n_messages + 1 :][:n_terms]
    messages = refs[n_messages + 1 + n_terms + n_before :][:n_messages]
    for k, message in enumerate(messages):
        message[0] = own[k][...]
        message[1] = swapped[k + 1]
    if n_terms:
        total = terms[0][...].astype(jnp.float32)
        for term in terms[1:]:
            total += term[...].astype(jnp.float32)
        refs[-1][...] = total


def merge(own, swapped, terms, before):
    n_messages = len(own)
    lat, n_rows = own[0].shape
    vmem = pl.BlockSpec(memory_space=pltpu.VMEM)
    outs = pl.pallas_call(
        functools.partial(merge_kernel, n_messages, len(terms), len(before)),
        out_shape=[jax.ShapeDtypeStruct((2, lat, n_rows), jnp.bfloat16)] * n_messages
        + [jax.ShapeDtypeStruct(term.shape, jnp.float32) for term in terms[:1]],
        in_specs=[vmem] * (n_messages + 1 + len(terms))
        + [pl.BlockSpec(memory_space=pl.ANY)] * len(before),
        out_specs=[vmem] * (n_messages + len(terms[:1])),
        compiler_params=pltpu.CompilerParams(vmem_limit_bytes=18 * 2**20),
        cost_estimate=cost(COST_T),
        name="merge",
    )(*own, swapped, *terms, *before)
    return list(outs[:n_messages]), list(outs[n_messages:])


def widen_kernel(count, scale, n_before, n_mem, place_ref, *refs):
    refs = refs[n_before:]
    lhs_ref, inc_ref = refs[-2:]
    outs, refs = refs[-2 - n_mem : -2], refs[: -2 - n_mem]
    parts, (own, swapped, lon_ref, perturb_ref) = refs[:-4], refs[-4:]
    n_pairs = len(parts) + 1
    group, times, lat, nlon = (perturb_ref.shape[i] for i in (0, 1, 3, 4))
    n_band, depth = 2 * n_pairs, 2 * LANE
    lon = nlon // n_band
    tail = lon - LANE
    n_fields = group * count
    level = pl.program_id(0)

    @pl.when(level == 0)
    def _():
        lhs_ref[...] = jnp.zeros_like(lhs_ref)

    for i in range(count):

        @pl.when(level == i)
        def _():
            for v in range(n_band):
                part = parts[v // 2 - 1].at[v % 2] if v > 1 else swapped.at[0] if v else own
                source = pl.multiple_of((place_ref[0] ^ v) * depth, depth)
                for s in range(group):
                    field = i * group + s
                    lhs_ref[s, :lat, pl.ds(source, LANE)] = part[
                        :, field * LANE : (field + 1) * LANE
                    ]
                    at = n_fields * LANE + field * tail
                    lhs_ref[s, :lat, pl.ds(source + LANE, tail)] = part[:, at : at + tail]

    rows = lhs_ref.shape[0] * lhs_ref.shape[1]
    reach, width = reach_of(nlon), 2 * LANE
    for start in range(0, nlon, width):
        stop = min(start + width, nlon)
        near = {(k % nlon) // lon for k in range(start - reach, stop + reach)}
        fields = jnp.zeros((rows, stop - start), jnp.float32)
        for j in sorted(near):
            fields += jnp.dot(
                lhs_ref[:, :, j * depth : (j + 1) * depth].reshape(rows, depth),
                lon_ref[j, :, start:stop],
                preferred_element_type=jnp.float32,
            )
        fields = fields.reshape(group, lhs_ref.shape[1], stop - start)[:, :lat]
        for t in range(times):
            total = perturb_ref[0, t, 0, :, start:stop].astype(jnp.float32) * fields[0]
            for s in range(1, group):
                total += perturb_ref[s, t, 0, :, start:stop].astype(jnp.float32) * fields[s]
            inc_ref[t, :, start:stop] = total * scale
    share = nlon // n_mem
    for w, out in enumerate(outs):
        for q in range(n_mem):

            @pl.when((place_ref[1] ^ w) == q)
            def _():
                for t in range(times):
                    out[t, 0] = inc_ref[t, :, q * share : (q + 1) * share].astype(out.dtype)


def widen(parts, own, swapped, place, lon_matrix, perturb, first, count, n_mem, scale, before, us):
    group, times, levels, lat, nlon = perturb.shape
    n_pairs, n_rows = len(parts) + 1, own.shape[1]
    share = nlon // n_mem
    once = pl.Buffered(1)
    return pl.pallas_call(
        functools.partial(widen_kernel, count, scale, len(before), n_mem),
        out_shape=[jax.ShapeDtypeStruct((times, count, lat, share), LINK)] * n_mem,
        grid=(count,),
        in_specs=[pl.BlockSpec(memory_space=pltpu.SMEM)]
        + [pl.BlockSpec(memory_space=pl.ANY)] * len(before)
        + [pl.BlockSpec((2, lat, n_rows), lambda i: (0, 0, 0), pipeline_mode=once)] * len(parts)
        + [
            pl.BlockSpec((lat, n_rows), lambda i: (0, 0), pipeline_mode=once),
            pl.BlockSpec((1, lat, n_rows), lambda i: (0, 0, 0), pipeline_mode=once),
            pl.BlockSpec(lon_matrix.shape, lambda i: (0, 0, 0), pipeline_mode=once),
            pl.BlockSpec((group, times, 1, lat, nlon), lambda i: (0, 0, first + i, 0, 0)),
        ],
        out_specs=[pl.BlockSpec((times, 1, lat, share), lambda i: (0, i, 0, 0))] * n_mem,
        scratch_shapes=[
            pltpu.VMEM((group, round_up(lat, 16), 4 * LANE * n_pairs), jnp.bfloat16),
            pltpu.VMEM((times, lat, nlon), jnp.float32),
        ],
        compiler_params=pltpu.CompilerParams(vmem_limit_bytes=26 * 2**20),
        cost_estimate=cost(us),
        name="lon_conv",
    )(place, *before, *parts, own, swapped, lon_matrix, perturb)


def plain_shards(control, perturb, loc_scales, member_of):
    lat_matrix = kernel_matrix(NLAT, loc_scales[0] * NLAT, False)
    lon_matrix = kernel_matrix(NLON, loc_scales[1] * NLON, True)
    along_lat = jnp.einsum(
        "mkla,ba->mklb", control, lat_matrix, preferred_element_type=jnp.float32
    ).astype(jnp.bfloat16)
    regrouped = lax.all_to_all(along_lat, "band", split_axis=3, concat_axis=1, tiled=True)
    widened = jnp.einsum("mkla,nk->mlan", regrouped, lon_matrix, preferred_element_type=jnp.float32)
    group_size = control.shape[0]
    members_all = member_of.shape[0]
    group_index = lax.axis_index("mem")
    own_members = (
        lax.dynamic_slice_in_dim(member_of, group_index * group_size, group_size, 0)
        - group_index * group_size
    )
    one_hot = (own_members[:, None] == jnp.arange(group_size, dtype=jnp.int32)[None, :]).astype(
        jnp.float32
    )
    slot_fields = jnp.einsum("sj,jlan->slan", one_hot, widened, precision=lax.Precision.HIGHEST)
    group_part = jnp.sum(perturb.astype(jnp.float32) * slot_fields[:, None], axis=0) / math.sqrt(
        members_all - 1
    )
    return lax.psum_scatter(group_part, "mem", scatter_dimension=3, tiled=True)


def swaps(size, mask):
    return [(i, i ^ mask) for i in range(size)]


def shards(n_mem, n_band, control, perturb, loc_scales, member_of):
    group, lon, levels, nlat = control.shape
    lat, nlon = perturb.shape[3:]
    n_pairs = n_band // 2
    scale = 1.0 / math.sqrt(member_of.shape[0] - 1)
    mem, band = lax.axis_index("mem"), lax.axis_index("band")
    own = lax.dynamic_slice_in_dim(member_of, mem * group, group, 0) - mem * group
    pairs = 2 * jnp.arange(n_pairs, dtype=jnp.int32)
    partner = jnp.concatenate([pairs, pairs + 1]) ^ band
    lat_rows = (partner[:, None] * lat + jnp.arange(lat, dtype=jnp.int32)[None, :]).reshape(-1)
    lat_matrix = kernel_entries(
        lat_rows, jnp.arange(nlat, dtype=jnp.int32), nlat, loc_scales[0] * nlat, False
    )
    chunks = chunks_of(levels)
    columns = jnp.arange(2 * LANE, dtype=jnp.int32)[None, :]
    sources = jnp.arange(n_band, dtype=jnp.int32)[:, None] * lon + columns
    lon_matrix = None
    prepared, arrived, made, done = [], [], [], [None] * len(chunks)
    queued = []
    ahead = 2
    place = jnp.stack([band, mem])
    for step in range(len(chunks) + ahead):
        c = step - ahead
        if step < len(chunks):
            before = queued[step - ahead][:1] if step >= ahead else []
            *own_parts, crossing = send_parts(
                control, own, lat_matrix, *chunks[step], n_pairs, before
            )
            prepared.append(own_parts)
            with jax.named_scope(f"cores_{step}"):
                swapped = lax.ppermute(crossing, "band", swaps(n_band, 1))
            early = step - ahead - 1
            messages, total = merge(
                own_parts[1:],
                swapped,
                made[early] if early >= 0 else [],
                arrived[step - ahead][0] if step >= ahead else [],
            )
            queued.append(messages)
            if early >= 0:
                done[early] = total[0]
            got = [None] * len(messages)
            for k in sorted(range(1, n_pairs), key=lambda k: -k):
                with jax.named_scope(f"chips_{step}_{k}"):
                    got[k - 1] = lax.ppermute(messages[k - 1], "band", swaps(n_band, 2 * k))
            arrived.append([got, own_parts[0], swapped])
        if c >= 0:
            if lon_matrix is None:
                scales, queued[1][0] = lax.optimization_barrier((loc_scales, queued[1][0]))
                lon_matrix = kernel_entries(
                    sources.reshape(-1),
                    jnp.arange(nlon, dtype=jnp.int32),
                    nlon,
                    scales[1] * nlon,
                    True,
                ).reshape(n_band, 2 * LANE, nlon)
                lon_matrix = jnp.where(columns[:, :, None] < lon, lon_matrix, jnp.bfloat16(0))
            before = queued[-1][:1]
            before = before + [terms[0] for terms in made[-1:]]
            shares = widen(
                *arrived[c], place, lon_matrix, perturb, *chunks[c], n_mem, scale, before,
                COST_L if c + 1 == len(chunks) else COST_R
            )
            terms = [shares[0]]
            for w in range(n_mem - 1, 0, -1):
                with jax.named_scope(f"mem_{c}_{w}"):
                    terms.append(lax.ppermute(shares[w], "mem", swaps(n_mem, w)))
            made.append(terms)
    for c, terms in enumerate(made):
        if done[c] is None:
            done[c] = sum(term.astype(jnp.float32) for term in terms)
    return jnp.concatenate(done, axis=1)


def solution(mesh):
    n_mem, n_band = mesh.shape["mem"], mesh.shape["band"]
    in_specs = (P("mem", "band", None, None), P("mem", None, None, "band", None), P(), P())
    out_specs = P(None, None, "band", "mem")
    rows, columns = NLAT // n_band, NLON // n_band
    fits = rows % 8 == 0 and LANE < columns <= 2 * LANE and columns % 4 == 0
    local = functools.partial(shards, n_mem, n_band) if fits else plain_shards
    return jax.shard_map(local, mesh=mesh, in_specs=in_specs, out_specs=out_specs, check_vma=False)
```

```python
import functools
import math

import jax
import jax.numpy as jnp
from jax import lax
from jax.experimental import pallas as pl
from jax.experimental.pallas import tpu as pltpu
from jax.sharding import PartitionSpec as P

NLAT = 704
NLON = 1440
LANE = 128
LINK = jnp.bfloat16
COST_S, COST_T, COST_R, COST_L = 1, 1, 1, 1


def cost(us):
    return pl.CostEstimate(flops=int(1e9 * us), bytes_accessed=0, transcendentals=0)


def kernel_entries(rows, columns, cells, spread, periodic):
    distance = jnp.abs(rows[:, None].astype(jnp.float32) - columns[None, :].astype(jnp.float32))
    if periodic:
        distance = jnp.minimum(distance, cells - distance)
    weights = jnp.exp(-0.5 * (distance / spread) ** 2) / jnp.sqrt(math.sqrt(math.pi) * spread)
    return weights.astype(jnp.bfloat16)


def kernel_matrix(cells, spread, periodic):
    index = jnp.arange(cells, dtype=jnp.int32)
    return kernel_entries(index, index, cells, spread, periodic)


def round_up(value, unit):
    return -(-value // unit) * unit


def chunks_of(levels):
    counts, left = [2], levels - 4
    while left:
        counts.append(min(3, left))
        left -= counts[-1]
    counts += [2]
    return [(sum(counts[:c]), count) for c, count in enumerate(counts)]


def reach_of(cells):
    return int(13.65 * cells / 256)


def send_kernel(first, count, base, n_before, own_ref, control_ref, lat_ref, *rest):
    rest = rest[n_before:]
    outs, (held, wide, rows_ref, sems) = rest[:-4], rest[-4:]
    group, lon, block = held.shape[0], held.shape[1], held.shape[2]
    lat, crossing = outs[0].shape[0], outs[-1]
    tail = lon - LANE
    n_fields = group * count
    copies = [
        pltpu.make_async_copy(
            control_ref.at[own_ref[s], :, pl.ds(base, block), :], held.at[s], sems.at[s]
        )
        for s in range(group)
    ]
    for copy in copies:
        copy.start()
    used = n_fields * lon
    if rows_ref.shape[0] > used:
        rows_ref[used:, :] = jnp.zeros((rows_ref.shape[0] - used, rows_ref.shape[1]), jnp.float32)
    for s in range(group):
        copies[s].wait()
        for at in range(0, held.shape[3], LANE):
            lanes = min(LANE, held.shape[3] - at)
            wide[:, :lanes] = held[s, :, :, at : at + lanes].astype(jnp.float32).reshape(
                lon * block, lanes
            )
            for i in range(count):
                field = i * group + s
                rows = wide[pl.ds(first - base + i, lon, stride=block), :][:, :lanes]
                rows_ref[pl.ds(field * LANE, LANE), at : at + lanes] = rows[:LANE]
                rows_ref[pl.ds(n_fields * LANE + field * tail, tail), at : at + lanes] = rows[LANE:]

    def columns(start, width):
        part = rows_ref[pl.ds(start, width), :].astype(jnp.bfloat16)
        product = lax.dot_general(
            lat_ref[...], part, (((1,), (1,)), ((), ())), preferred_element_type=jnp.float32
        )
        for k, out in enumerate(outs[:-1]):
            out[:, pl.ds(start, width)] = product[k * lat : (k + 1) * lat].astype(jnp.bfloat16)
            at = (len(outs) - 1 + k) * lat
            crossing[k, :, pl.ds(start, width)] = product[at : at + lat].astype(jnp.bfloat16)

    width = 2 * LANE
    whole = rows_ref.shape[0] // width

    @pl.loop(0, whole)
    def _(step):
        columns(pl.multiple_of(step * width, width), width)

    if rows_ref.shape[0] % width:
        columns(whole * width, rows_ref.shape[0] % width)


def send_parts(control, own, lat_matrix, first, count, n_pairs, before):
    group, lon, levels, nlat = control.shape
    lat, unit = nlat // (2 * n_pairs), 8
    base = first // unit * unit
    block = round_up(first + count, unit) - base
    n_rows = round_up(group * count * lon, LANE)
    return pl.pallas_call(
        functools.partial(send_kernel, first, count, base, len(before)),
        out_shape=[jax.ShapeDtypeStruct((lat, n_rows), jnp.bfloat16)] * n_pairs
        + [jax.ShapeDtypeStruct((n_pairs, lat, n_rows), jnp.bfloat16)],
        in_specs=[
            pl.BlockSpec(memory_space=pltpu.SMEM),
            pl.BlockSpec(memory_space=pl.ANY),
            pl.BlockSpec(memory_space=pltpu.VMEM),
        ]
        + [pl.BlockSpec(memory_space=pl.ANY)] * len(before),
        out_specs=[pl.BlockSpec(memory_space=pltpu.VMEM)] * (n_pairs + 1),
        scratch_shapes=[
            pltpu.VMEM((group, lon, block, nlat), jnp.bfloat16),
            pltpu.VMEM((lon * block, LANE), jnp.float32),
            pltpu.VMEM((n_rows, nlat), jnp.float32),
            pltpu.SemaphoreType.DMA((group,)),
        ],
        compiler_params=pltpu.CompilerParams(vmem_limit_bytes=56 * 2**20),
        cost_estimate=cost(COST_S),
        name="lat_conv",
    )(own, control, lat_matrix, *before)


def merge_kernel(n_messages, n_terms, n_before, *refs):
    own, swapped, terms = refs[:n_messages], refs[n_messages], refs[n_messages + 1 :][:n_terms]
    messages = refs[n_messages + 1 + n_terms + n_before :][:n_messages]
    for k, message in enumerate(messages):
        message[0] = own[k][...]
        message[1] = swapped[k + 1]
    if n_terms:
        total = terms[0][...].astype(jnp.float32)
        for term in terms[1:]:
            total += term[...].astype(jnp.float32)
        refs[-1][...] = total


def merge(own, swapped, terms, before):
    n_messages = len(own)
    lat, n_rows = own[0].shape
    vmem = pl.BlockSpec(memory_space=pltpu.VMEM)
    outs = pl.pallas_call(
        functools.partial(merge_kernel, n_messages, len(terms), len(before)),
        out_shape=[jax.ShapeDtypeStruct((2, lat, n_rows), jnp.bfloat16)] * n_messages
        + [jax.ShapeDtypeStruct(term.shape, jnp.float32) for term in terms[:1]],
        in_specs=[vmem] * (n_messages + 1 + len(terms))
        + [pl.BlockSpec(memory_space=pl.ANY)] * len(before),
        out_specs=[vmem] * (n_messages + len(terms[:1])),
        compiler_params=pltpu.CompilerParams(vmem_limit_bytes=40 * 2**20),
        cost_estimate=cost(COST_T),
        name="merge",
    )(*own, swapped, *terms, *before)
    return list(outs[:n_messages]), list(outs[n_messages:])


def widen_kernel(count, scale, n_before, n_mem, place_ref, *refs):
    refs = refs[n_before:]
    lhs_ref, inc_ref = refs[-2:]
    outs, refs = refs[-2 - n_mem : -2], refs[: -2 - n_mem]
    parts, (own, swapped, lon_ref, perturb_ref) = refs[:-4], refs[-4:]
    n_pairs = len(parts) + 1
    group, times, lat, nlon = (perturb_ref.shape[i] for i in (0, 1, 3, 4))
    n_band, depth = 2 * n_pairs, 2 * LANE
    lon = nlon // n_band
    tail = lon - LANE
    n_fields = group * count
    level = pl.program_id(0)

    @pl.when(level == 0)
    def _():
        lhs_ref[...] = jnp.zeros_like(lhs_ref)

    for i in range(count):

        @pl.when(level == i)
        def _():
            for v in range(n_band):
                part = parts[v // 2 - 1].at[v % 2] if v > 1 else swapped.at[0] if v else own
                source = pl.multiple_of((place_ref[0] ^ v) * depth, depth)
                for s in range(group):
                    field = i * group + s
                    lhs_ref[s, :lat, pl.ds(source, LANE)] = part[
                        :, field * LANE : (field + 1) * LANE
                    ]
                    at = n_fields * LANE + field * tail
                    lhs_ref[s, :lat, pl.ds(source + LANE, tail)] = part[:, at : at + tail]

    rows = lhs_ref.shape[0] * lhs_ref.shape[1]
    reach, width = reach_of(nlon), 2 * LANE
    for start in range(0, nlon, width):
        stop = min(start + width, nlon)
        near = {(k % nlon) // lon for k in range(start - reach, stop + reach)}
        fields = jnp.zeros((rows, stop - start), jnp.float32)
        for j in sorted(near):
            fields += jnp.dot(
                lhs_ref[:, :, j * depth : (j + 1) * depth].reshape(rows, depth),
                lon_ref[j, :, start:stop],
                preferred_element_type=jnp.float32,
            )
        fields = fields.reshape(group, lhs_ref.shape[1], stop - start)[:, :lat]
        for t in range(times):
            total = perturb_ref[0, t, 0, :, start:stop].astype(jnp.float32) * fields[0]
            for s in range(1, group):
                total += perturb_ref[s, t, 0, :, start:stop].astype(jnp.float32) * fields[s]
            inc_ref[t, :, start:stop] = total * scale
    share = nlon // n_mem
    for w, out in enumerate(outs):
        for q in range(n_mem):

            @pl.when((place_ref[1] ^ w) == q)
            def _():
                for t in range(times):
                    out[t, 0] = inc_ref[t, :, q * share : (q + 1) * share].astype(out.dtype)


def widen(parts, own, swapped, place, lon_matrix, perturb, first, count, n_mem, scale, before, us):
    group, times, levels, lat, nlon = perturb.shape
    n_pairs, n_rows = len(parts) + 1, own.shape[1]
    share = nlon // n_mem
    once = pl.Buffered(1)
    return pl.pallas_call(
        functools.partial(widen_kernel, count, scale, len(before), n_mem),
        out_shape=[jax.ShapeDtypeStruct((times, count, lat, share), LINK)] * n_mem,
        grid=(count,),
        in_specs=[pl.BlockSpec(memory_space=pltpu.SMEM)]
        + [pl.BlockSpec(memory_space=pl.ANY)] * len(before)
        + [pl.BlockSpec((2, lat, n_rows), lambda i: (0, 0, 0), pipeline_mode=once)] * len(parts)
        + [
            pl.BlockSpec((lat, n_rows), lambda i: (0, 0), pipeline_mode=once),
            pl.BlockSpec((1, lat, n_rows), lambda i: (0, 0, 0), pipeline_mode=once),
            pl.BlockSpec(lon_matrix.shape, lambda i: (0, 0, 0), pipeline_mode=once),
            pl.BlockSpec((group, times, 1, lat, nlon), lambda i: (0, 0, first + i, 0, 0)),
        ],
        out_specs=[pl.BlockSpec((times, 1, lat, share), lambda i: (0, i, 0, 0))] * n_mem,
        scratch_shapes=[
            pltpu.VMEM((group, round_up(lat, 16), 4 * LANE * n_pairs), jnp.bfloat16),
            pltpu.VMEM((times, lat, nlon), jnp.float32),
        ],
        compiler_params=pltpu.CompilerParams(vmem_limit_bytes=56 * 2**20),
        cost_estimate=cost(us),
        name="lon_conv",
    )(place, *before, *parts, own, swapped, lon_matrix, perturb)


def plain_shards(control, perturb, loc_scales, member_of):
    lat_matrix = kernel_matrix(NLAT, loc_scales[0] * NLAT, False)
    lon_matrix = kernel_matrix(NLON, loc_scales[1] * NLON, True)
    along_lat = jnp.einsum(
        "mkla,ba->mklb", control, lat_matrix, preferred_element_type=jnp.float32
    ).astype(jnp.bfloat16)
    regrouped = lax.all_to_all(along_lat, "band", split_axis=3, concat_axis=1, tiled=True)
    widened = jnp.einsum("mkla,nk->mlan", regrouped, lon_matrix, preferred_element_type=jnp.float32)
    group_size = control.shape[0]
    members_all = member_of.shape[0]
    group_index = lax.axis_index("mem")
    own_members = (
        lax.dynamic_slice_in_dim(member_of, group_index * group_size, group_size, 0)
        - group_index * group_size
    )
    one_hot = (own_members[:, None] == jnp.arange(group_size, dtype=jnp.int32)[None, :]).astype(
        jnp.float32
    )
    slot_fields = jnp.einsum("sj,jlan->slan", one_hot, widened, precision=lax.Precision.HIGHEST)
    group_part = jnp.sum(perturb.astype(jnp.float32) * slot_fields[:, None], axis=0) / math.sqrt(
        members_all - 1
    )
    return lax.psum_scatter(group_part, "mem", scatter_dimension=3, tiled=True)


def swaps(size, mask):
    return [(i, i ^ mask) for i in range(size)]


def shards(n_mem, n_band, control, perturb, loc_scales, member_of):
    group, lon, levels, nlat = control.shape
    lat, nlon = perturb.shape[3:]
    n_pairs = n_band // 2
    scale = 1.0 / math.sqrt(member_of.shape[0] - 1)
    mem, band = lax.axis_index("mem"), lax.axis_index("band")
    own = lax.dynamic_slice_in_dim(member_of, mem * group, group, 0) - mem * group
    pairs = 2 * jnp.arange(n_pairs, dtype=jnp.int32)
    partner = jnp.concatenate([pairs, pairs + 1]) ^ band
    lat_rows = (partner[:, None] * lat + jnp.arange(lat, dtype=jnp.int32)[None, :]).reshape(-1)
    lat_matrix = kernel_entries(
        lat_rows, jnp.arange(nlat, dtype=jnp.int32), nlat, loc_scales[0] * nlat, False
    )
    chunks = chunks_of(levels)
    columns = jnp.arange(2 * LANE, dtype=jnp.int32)[None, :]
    sources = jnp.arange(n_band, dtype=jnp.int32)[:, None] * lon + columns
    lon_matrix = None
    prepared, arrived, made, done = [], [], [], [None] * len(chunks)
    queued = []
    ahead = 2
    place = jnp.stack([band, mem])
    for step in range(len(chunks) + ahead):
        c = step - ahead
        if step < len(chunks):
            before = queued[step - ahead][:1] if step >= ahead else []
            *own_parts, crossing = send_parts(
                control, own, lat_matrix, *chunks[step], n_pairs, before
            )
            prepared.append(own_parts)
            with jax.named_scope(f"cores_{step}"):
                swapped = lax.ppermute(crossing, "band", swaps(n_band, 1))
            early = step - ahead - 1
            messages, total = merge(
                own_parts[1:],
                swapped,
                made[early] if early >= 0 else [],
                arrived[step - ahead][0] if step >= ahead else [],
            )
            queued.append(messages)
            if early >= 0:
                done[early] = total[0]
            got = [None] * len(messages)
            for k in sorted(range(1, n_pairs), key=lambda k: -k):
                with jax.named_scope(f"chips_{step}_{k}"):
                    got[k - 1] = lax.ppermute(messages[k - 1], "band", swaps(n_band, 2 * k))
            arrived.append([got, own_parts[0], swapped])
        if c >= 0:
            if lon_matrix is None:
                scales, queued[1][0] = lax.optimization_barrier((loc_scales, queued[1][0]))
                lon_matrix = kernel_entries(
                    sources.reshape(-1),
                    jnp.arange(nlon, dtype=jnp.int32),
                    nlon,
                    scales[1] * nlon,
                    True,
                ).reshape(n_band, 2 * LANE, nlon)
                lon_matrix = jnp.where(columns[:, :, None] < lon, lon_matrix, jnp.bfloat16(0))
            before = queued[-1][:1]
            before = before + [terms[0] for terms in made[-1:]]
            shares = widen(
                *arrived[c], place, lon_matrix, perturb, *chunks[c], n_mem, scale, before,
                COST_L if c + 1 == len(chunks) else COST_R
            )
            terms = [shares[0]]
            for w in range(n_mem - 1, 0, -1):
                with jax.named_scope(f"mem_{c}_{w}"):
                    terms.append(lax.ppermute(shares[w], "mem", swaps(n_mem, w)))
            made.append(terms)
    for c, terms in enumerate(made):
        if done[c] is None:
            done[c] = sum(term.astype(jnp.float32) for term in terms)
    return jnp.concatenate(done, axis=1)


def solution(mesh):
    n_mem, n_band = mesh.shape["mem"], mesh.shape["band"]
    in_specs = (P("mem", "band", None, None), P("mem", None, None, "band", None), P(), P())
    out_specs = P(None, None, "band", "mem")
    rows, columns = NLAT // n_band, NLON // n_band
    fits = rows % 8 == 0 and LANE < columns <= 2 * LANE and columns % 4 == 0
    local = functools.partial(shards, n_mem, n_band) if fits else plain_shards
    return jax.shard_map(local, mesh=mesh, in_specs=in_specs, out_specs=out_specs, check_vma=False)
```
